32 devices in a mesh: tok: 2 (over core), head: 4 (over y, x), exp: 4 (over z).
Axes of the slice: x: 2, y: 2, z: 4, core: 2. Of those that a mesh axis runs over, the one named last changes fastest.
Arguments:
- context: bfloat16 [4, 64, 4096], P('exp', 'tok', 'head'), may hold values from -6 to 6
- out_proj: bfloat16 [4096, 4096], P('head', 'exp'), may hold values from -0.125 to 0.125
- stream: float32 [4, 64, 4096], P('exp', 'tok', 'head'), may hold values from -75 to 75
- norm_gain: float32 [4096], replicated, may hold values from 0.1 to 1.9
- expert_ids: int32 [4, 64, 8], P('exp', 'tok'), may hold values from 0 to 31, as said below
- slot_ids: int32 [4, 64, 8], P('exp', 'tok'), may hold values from -1 to 11, as said below
- gate_probs: float32 [4, 64, 8], P('exp', 'tok'), may hold values from 0.02 to 0.3
- w_gate: bfloat16 [32, 3072, 4096], P(('tok', 'exp'), 'head'), may hold values from -0.09375 to 0.09375
- w_up: bfloat16 [32, 3072, 4096], P(('tok', 'exp'), 'head'), may hold values from -0.09375 to 0.09375
- w_down: bfloat16 [32, 3072, 4096], P(('tok', 'exp'), 'head'), may hold values from -0.15625 to 0.15625
Outputs:
- mixed: float32 [4, 64, 4096], P('exp', 'tok', 'head')
The draws below stay inside these ranges and needn't reach their ends.
Inputs may be any that keep to these rules, and one draw needn't show every extreme that they name: `expert_ids`: each token names 8 different experts. `slot_ids`: within a block of 32 consecutive tokens of one image, the choices of one expert take slots 0, 1, 2, ... in token order until its 12 slots are full, later ones get -1; in every block some expert fills all 12 slots.
All inputs are finite; a program needn't handle non-finite values.
Results may differ from the reference program's by a relative error of at most 0.0034.
Values may be sent and summed in bfloat16 or wider, within the bound.
A program may use at most 128 MiB of HBM per device.

```python
import jax
import jax.numpy as jnp
from jax import lax

D = 4096
HID = 3072
EXPERTS = 32
TOP = 8
TOK_DEV = 32
CAP = 12
IMAGES = 4
SEQ = 64
N_HEAD = 4


def routing_table(key):
    base_key = jax.random.fold_in(key, 4242)
    key_pop, key_noise, key_hot, key_rows = jax.random.split(base_key, 4)
    block_count = IMAGES * SEQ // TOK_DEV
    popular = jax.random.randint(key_pop, (EXPERTS,), 0, 64) ** 2
    noise = jax.random.randint(key_noise, (block_count, TOK_DEV, EXPERTS), 0, 4096)
    hot_expert = jax.random.randint(key_hot, (), 0, EXPERTS)
    row_keys = jax.random.split(key_rows, block_count)
    orders = jax.vmap(lambda one_key: jax.random.permutation(one_key, TOK_DEV))(row_keys)
    places = jnp.argsort(orders, axis=1, stable=True)
    forced = (places < CAP).astype(jnp.int32)
    expert_range = jnp.arange(EXPERTS, dtype=jnp.int32)
    is_hot = (expert_range == hot_expert).astype(jnp.int32)
    score = noise + popular[None, None, :] + forced[:, :, None] * is_hot[None, None, :] * 1048576
    distinct = score * EXPERTS + expert_range[None, None, :]
    chosen = lax.top_k(distinct, TOP)[1].astype(jnp.int32)
    one_hot = jnp.sum((chosen[:, :, :, None] == expert_range).astype(jnp.int32), axis=2)
    before = jnp.cumsum(one_hot, axis=1) - one_hot
    ranked = jnp.take_along_axis(before, chosen, axis=2)
    slots = jnp.where(ranked < CAP, ranked, -1).astype(jnp.int32)
    return (chosen.reshape(IMAGES, SEQ, TOP), slots.reshape(IMAGES, SEQ, TOP))


def draw_expert_ids(key, part):
    return routing_table(key)[0]


def draw_slot_ids(key, part):
    return routing_table(key)[1]


def draw_stream(key, part):
    key_base, key_cols, key_rows = jax.random.split(jax.random.fold_in(key, 99), 3)
    col_pos = jnp.arange(D, dtype=jnp.float32) / D
    col_scale = jnp.exp(jnp.log(10.0) * col_pos) * jax.random.uniform(key_cols, (D,), jnp.float32, 0.5, 1.5)
    row_scale = jnp.exp(jnp.log(10.0) * jax.random.uniform(key_rows, (IMAGES, SEQ, 1), jnp.float32))
    values = jnp.clip(jax.random.normal(key_base, (IMAGES, SEQ, D), jnp.float32), -4.0, 4.0)
    return values * col_scale * row_scale / 8.0


def raised(drawn, key, source, target, shards_of, factor):
    owner, partner = [(jnp.arange(drawn.shape[axis_at]) // (drawn.shape[axis_at] // shards_of)).reshape([-1 if axis == axis_at else 1 for axis in range(drawn.ndim)]) for axis_at in (source, target)]
    chosen = jax.random.permutation(key, shards_of)[partner]
    strong = (owner == chosen) | (owner == (partner + shards_of // 2) % shards_of)
    return jnp.where(strong, factor * drawn, drawn)


def shard_levels(stream_key, shape, pieces, least, largest):
    factor_of, own = 1.0, jax.random.fold_in(stream_key, 6)
    for axis_at, shards_of in pieces:
        steps = jnp.exp(jax.random.uniform(jax.random.fold_in(own, axis_at), (shards_of,), jnp.float32, least / len(pieces), largest / len(pieces)))
        factor_of = factor_of * jnp.repeat(steps, shape[axis_at] // shards_of).reshape([-1 if axis == axis_at else 1 for axis in range(len(shape))])
    return factor_of


def scatter_about(own_key, shape, scale, most, cuts=(), kind=jnp.bfloat16):
    loudness = shard_levels(own_key, shape, cuts, -0.22, 0.18) if cuts else 1.0
    values = jax.random.normal(own_key, shape, jnp.float32) * scale * loudness
    return jnp.minimum(jnp.maximum(values, -most), most).astype(kind)


def gaussian_with(stream_key, extent, deviation, reach, shards, heavy, kind=jnp.bfloat16):
    drawn = deviation * jax.random.normal(stream_key, extent, jnp.float32)
    if shards:
        drawn = drawn * shard_levels(stream_key, extent, shards, -0.22, 0.18)
    return jnp.clip(raised(drawn, jax.random.fold_in(stream_key, 3), *heavy), -reach, reach).astype(kind)


def setup_inputs(seed: int = 0) -> dict:
    key_of = jax.random.split(jax.random.key(seed), 11)
    context = scatter_about(key_of[0], (IMAGES, SEQ, D), 1.0, 6.0, ((0, 4), (1, 2), (2, 4)))
    out_proj = gaussian_with(key_of[1], (D, D), D ** -0.5, 0.125, ((0, 4), (1, 4)), (0, 1, 4, 2.0))
    stream = draw_stream(jax.random.fold_in(key_of[10], 71), 0)
    norm_gain = jnp.clip(1.0 + 0.18 * jax.random.normal(key_of[3], (D,), jnp.float32), 0.1, 1.9)
    expert_ids = draw_expert_ids(jax.random.fold_in(key_of[10], 71), 0)
    slot_ids = draw_slot_ids(jax.random.fold_in(key_of[10], 71), 0)
    gate_probs = jnp.clip(0.02 + 0.28 * jax.random.uniform(key_of[6], (IMAGES, SEQ, TOP), jnp.float32) ** shard_levels(key_of[6], (IMAGES, SEQ, TOP), ((0, 4), (1, 2)), -0.2, 0.2), 0.02, 0.3)
    w_gate = scatter_about(key_of[7], (EXPERTS, HID, D), D ** -0.5, 0.09375, ((0, 8), (1, 4)))
    w_up = scatter_about(key_of[8], (EXPERTS, HID, D), D ** -0.5, 0.09375, ((0, 8), (1, 4)))
    w_down = gaussian_with(key_of[9], (EXPERTS, HID, D), HID ** -0.5, 0.15625, ((0, 8), (1, 4)), (1, 2, 4, 2.0))
    return {"context": context, "out_proj": out_proj, "stream": stream, "norm_gain": norm_gain, "expert_ids": expert_ids, "slot_ids": slot_ids, "gate_probs": gate_probs, "w_gate": w_gate, "w_up": w_up, "w_down": w_down}


eps_value = 1e-05

def reference(context, out_proj, stream, norm_gain, expert_ids, slot_ids, gate_probs, w_gate, w_up, w_down):
    token_count = IMAGES * SEQ
    block_count = token_count // TOK_DEV
    flat_context = context.reshape(token_count, D)
    resid_mid = stream.reshape(token_count, D) + jnp.dot(flat_context, out_proj, preferred_element_type=jnp.float32)
    mean_sq = lax.optimization_barrier(jnp.mean(resid_mid * resid_mid, axis=1, keepdims=True))
    normed = (resid_mid * lax.rsqrt(mean_sq + eps_value) * norm_gain).astype(jnp.bfloat16)
    choice_ids = expert_ids.reshape(token_count, TOP).astype(jnp.int32)
    choice_slots = slot_ids.reshape(token_count, TOP).astype(jnp.int32)
    weights = gate_probs.reshape(token_count, TOP)
    block_of = (jnp.arange(token_count, dtype=jnp.int32) // TOK_DEV)[:, None]
    spill_slot = EXPERTS * block_count * CAP
    target = jnp.where(choice_slots >= 0, (choice_ids * block_count + block_of) * CAP + choice_slots, spill_slot).astype(jnp.int32)
    buffer_rows = jnp.zeros((spill_slot + 1, D), jnp.bfloat16).at[target.reshape(-1)].set(jnp.repeat(normed, TOP, axis=0))
    dispatched = buffer_rows[:spill_slot].reshape(EXPERTS, block_count * CAP, D)

    def expert_hidden(operands):
        inputs, gate_mat, up_mat = operands
        gate_part = jnp.dot(inputs, gate_mat.T, preferred_element_type=jnp.float32)
        up_part = jnp.dot(inputs, up_mat.T, preferred_element_type=jnp.float32)
        return (jax.nn.silu(gate_part) * up_part).astype(jnp.bfloat16)
    hidden = lax.map(expert_hidden, (dispatched, w_gate, w_up))
    slice_width = HID // N_HEAD

    def add_slice(index, total):
        first = index * slice_width
        hidden_slice = lax.dynamic_slice_in_dim(hidden, first, slice_width, 2).astype(jnp.float32)
        down_slice = lax.dynamic_slice_in_dim(w_down, first, slice_width, 1).astype(jnp.float32)
        part = jnp.einsum('erh,ehd->erd', hidden_slice, down_slice, precision=lax.Precision.HIGHEST).astype(jnp.bfloat16)
        lookup = jnp.concatenate([part.reshape(spill_slot, D), jnp.zeros((1, D), jnp.bfloat16)], axis=0)
        picked = lookup[target]
        return total + lax.optimization_barrier(jnp.sum(picked.astype(jnp.float32) * weights[:, :, None], axis=1))
    expert_mix = lax.fori_loop(0, N_HEAD, add_slice, jnp.zeros((token_count, D), jnp.float32))
    return (resid_mid + expert_mix).reshape(IMAGES, SEQ, D)
```

```python
import functools

import jax
import jax.numpy as jnp
from jax import lax
from jax.experimental import pallas as pl
from jax.experimental.pallas import tpu as pltpu
from jax.sharding import PartitionSpec as P

MESH = pl.DeviceIdType.MESH
LANES = 128
SLOT_BYTES = 50_400_000
F32 = jnp.float32
BF16 = jnp.bfloat16
eps_value = 1e-05


def kernel(
    n_tok, n_head, n_exp, n_slots,
    ctx_ref, proj_hbm, stream_ref, gain_ref, ids_ref, slots_ref, probs_ref,
    wg_hbm, wu_hbm, wd_hbm,
    out_ref,
    proj, wbuf, ctx_all, wall, stream_bf, stream_t, pbf, pown, prs,
    attn_buf, attn_in, ssq, x, hid, acc, obf, tin, hsend, hrecv, zsend, zrecv,
    proj_sem, w_sem, ctx_s, ctx_r, wz_s, wz_r, wt_s, wt_r, st_s, st_r,
    prs_s, prs_r, at_s, at_r, xz_s, xz_r, qz_s, qz_r, xh_s, xh_r, qh_s, qh_r,
    xt_s, xt_r, qt_s, qt_r, to_s, to_r, ho_s, ho_r, zo_s, zo_r,
):
    t, h, e = lax.axis_index("tok"), lax.axis_index("head"), lax.axis_index("exp")
    rows, width = stream_ref.shape
    n_local, n_hid, model = wg_hbm.shape
    tokens = n_tok * n_exp * rows
    tp = 1 - t
    turned = {"tok": t, "head": e, "exp": h}
    mine = h == e

    def send(src, dst, s_sem, r_sem, device):
        return pltpu.make_async_remote_copy(
            src_ref=src, dst_ref=dst, send_sem=s_sem, recv_sem=r_sem,
            device_id=device, device_id_type=MESH,
        )

    def on_exp(k):
        return {"exp": lax.rem(e + k, n_exp)}

    def on_head(k):
        return {"head": lax.rem(h + k, n_head)}

    on_tok = {"tok": tp}

    sources = (wg_hbm, wu_hbm, wd_hbm)

    def w_copy(q):
        return pltpu.make_async_copy(
            sources[q % 3].at[q // 3], wbuf.at[q % n_slots], w_sem.at[q % n_slots]
        )

    proj_copy = pltpu.make_async_copy(proj_hbm, proj, proj_sem)
    proj_copy.start()

    barrier = pltpu.get_barrier_semaphore()
    for k in range(1, n_exp):
        pl.semaphore_signal(barrier, inc=1, device_id=on_exp(k), device_id_type=MESH)
    for k in range(1, n_head):
        pl.semaphore_signal(barrier, inc=1, device_id=on_head(k), device_id_type=MESH)
    pl.semaphore_signal(barrier, inc=1, device_id=on_tok, device_id_type=MESH)

    @pl.when(jnp.logical_not(mine))
    def _():
        pl.semaphore_signal(barrier, inc=1, device_id=turned, device_id_type=MESH)

    for q in range(n_slots):
        w_copy(q).start()
    stream_bf[...] = stream_ref[...].astype(BF16)
    lane = lax.broadcasted_iota(jnp.int32, (rows, LANES), 1)
    dense = jnp.zeros((rows, LANES), F32)
    for k in range(ids_ref.shape[1]):
        hit = (ids_ref[:, k : k + 1] == lane) & (slots_ref[:, k : k + 1] >= 0)
        dense = dense + jnp.where(hit, probs_ref[:, k : k + 1], 0.0)
    wall[t, e] = dense
    ctx_all[e] = ctx_ref[...]

    @pl.when(mine)
    def _():
        pl.semaphore_wait(barrier, n_exp - 1 + n_head - 1 + 1)

    @pl.when(jnp.logical_not(mine))
    def _():
        pl.semaphore_wait(barrier, n_exp - 1 + n_head - 1 + 2)

    ctx_c = [
        send(ctx_ref, ctx_all.at[e], ctx_s.at[k], ctx_r.at[k], on_exp(k)) for k in range(1, n_exp)
    ]
    for c in ctx_c:
        c.start()
    stream_c = send(stream_bf, stream_t, st_s, st_r, turned)

    @pl.when(jnp.logical_not(mine))
    def _():
        stream_c.start()

    wz_c = [
        send(wall.at[t, e], wall.at[t, e], wz_s.at[k], wz_r.at[k], on_exp(k))
        for k in range(1, n_exp)
    ]
    for c in wz_c:
        c.start()
    proj_copy.wait()
    for c in ctx_c:
        c.wait()

    tile = min(width, 256)

    def project(i, carry):
        cols = pl.ds(pl.multiple_of(i * tile, tile), tile)
        part = jnp.dot(
            ctx_all[...].reshape(n_exp * rows, ctx_ref.shape[1]), proj[:, cols],
            preferred_element_type=F32,
        ).reshape(n_exp, rows, tile)
        pown[:, :, cols] = part
        pbf[:, :, cols] = part.astype(BF16)
        return carry

    lax.fori_loop(0, proj.shape[1] // tile, project, 0)
    prs_c = [
        send(
            pbf.at[lax.rem(h + k, n_head)], prs.at[k - 1], prs_s.at[k], prs_r.at[k], on_head(k)
        )
        for k in range(1, n_head)
    ]
    for c in prs_c:
        c.start()
    for c in wz_c:
        c.wait()
    wt_c = send(wall.at[t], wall.at[t], wt_s, wt_r, on_tok)
    wt_c.start()

    @pl.when(jnp.logical_not(mine))
    def _():
        stream_c.wait()

    @pl.when(mine)
    def _():
        stream_t[...] = stream_bf[...]

    for c in prs_c:
        c.wait()
    attn = pown[h]
    for k in range(1, n_head):
        attn = attn + prs[k - 1].astype(F32)
    attn_buf[...] = attn
    attn_c = send(attn_buf, attn_in, at_s, at_r, turned)

    resid = attn + stream_t[...].astype(F32)
    gain = gain_ref[:, pl.ds(pl.multiple_of(e * width, LANES), width)]
    own_cols = pl.ds(pl.multiple_of(e * width, LANES), width)
    x[t, h, :, own_cols] = (resid * gain).astype(BF16)
    square = jnp.sum(resid * resid, axis=1, keepdims=True)
    row_id = lax.broadcasted_iota(jnp.int32, (rows, LANES), 0)
    flat = jnp.sum(jnp.where(row_id == lane, square, 0.0), axis=0, keepdims=True)
    ssq[t, h, e] = jnp.broadcast_to(flat, (8, LANES))

    def x_at(i, c):
        return x.at[t, i, :, pl.ds(pl.multiple_of(c * width, LANES), width)]

    xz_c = [
        send(x_at(h, e), x_at(h, e), xz_s.at[k], xz_r.at[k], on_exp(k)) for k in range(1, n_exp)
    ]
    qz_c = [
        send(ssq.at[t, h, e], ssq.at[t, h, e], qz_s.at[k], qz_r.at[k], on_exp(k))
        for k in range(1, n_exp)
    ]
    for a, b in zip(xz_c, qz_c):
        a.start()
        b.start()
    xh_c = []
    for j in range(n_exp):
        if j:
            xz_c[j - 1].wait_recv()
        piece = lax.rem(e - j + n_exp, n_exp)
        for k in range(1, n_head):
            c = send(x_at(h, piece), x_at(h, piece), xh_s.at[k, j], xh_r.at[k, j], on_head(k))
            c.start()
            xh_c.append((k, j, c))
    for c in qz_c:
        c.wait_recv()
    qh_c = [
        send(ssq.at[t, h], ssq.at[t, h], qh_s.at[k], qh_r.at[k], on_head(k))
        for k in range(1, n_head)
    ]
    for c in qh_c:
        c.start()

    @pl.when(jnp.logical_not(mine))
    def _():
        attn_c.start()

    xt_c = []
    for k in range(n_head):
        if k:
            for kk, j, c in xh_c:
                if kk == k:
                    c.wait_recv()
            qh_c[k - 1].wait_recv()
        image = lax.rem(h - k + n_head, n_head)
        a = send(x.at[t, image], x.at[t, image], xt_s.at[k], xt_r.at[k], on_tok)
        b = send(ssq.at[t, image], ssq.at[t, image], qt_s.at[k], qt_r.at[k], on_tok)
        a.start()
        b.start()
        xt_c += [a, b]
    for c in xt_c:
        c.wait_recv()
    wt_c.wait()

    total = jnp.sum(ssq[...], axis=2)[:, :, 0:1, :]
    wide = jnp.broadcast_to(
        total, (n_tok, n_exp, rows, LANES)
    ).reshape(tokens, LANES)
    token_row = lax.rem(lax.broadcasted_iota(jnp.int32, (tokens, LANES), 0), rows)
    token_lane = lax.broadcasted_iota(jnp.int32, (tokens, LANES), 1)
    sums = jnp.sum(jnp.where(token_row == token_lane, wide, 0.0), axis=1, keepdims=True)
    scale = lax.rsqrt(sums / model + eps_value)
    weights = wall[...].reshape(tokens, LANES)

    hid_tile = 256 if n_hid % 256 == 0 else n_hid
    col_tile = min(width, 512)
    per = width // col_tile

    def expert(j):
        for m in range(2):
            w_copy(3 * j + m).wait()
        gs, us, ds_ = (3 * j) % n_slots, (3 * j + 1) % n_slots, (3 * j + 2) % n_slots
        number = (t * n_exp + e) * n_local + j
        gate_w = jnp.sum(jnp.where(token_lane == number, weights, 0.0), axis=1, keepdims=True)

        def up(i, carry):
            span = pl.ds(pl.multiple_of(i * hid_tile, hid_tile), hid_tile)
            dims = (((1,), (1,)), ((), ()))
            xv = x[...].reshape(tokens, model)
            g = lax.dot_general(xv, wbuf[gs, span, :], dims, preferred_element_type=F32) * scale
            u = lax.dot_general(xv, wbuf[us, span, :], dims, preferred_element_type=F32) * scale
            value = g / (1.0 + jnp.exp(-g)) * u * gate_w
            hid[i] = value.astype(BF16)
            return carry

        lax.fori_loop(0, n_hid // hid_tile, up, 0)
        for m in range(2):
            if 3 * j + m + n_slots < 3 * n_local:
                w_copy(3 * j + m + n_slots).start()
        w_copy(3 * j + 2).wait()

        def down(cols):
            value = jnp.zeros((tokens, col_tile), F32)
            for i in range(n_hid // hid_tile):
                value = value + jnp.dot(
                    hid[i], wbuf[ds_, i * hid_tile : (i + 1) * hid_tile, cols],
                    preferred_element_type=F32,
                )
            value = value.reshape(n_tok, n_exp, rows, col_tile)
            if j:
                value = value + acc[:, :, :, cols]
            acc[:, :, :, cols] = value

        return down

    to_c = []
    for j in range(n_local):
        down = expert(j)
        if j < n_local - 1:

            def step(i, carry):
                down(pl.ds(pl.multiple_of(i * col_tile, col_tile), col_tile))
                return carry

            lax.fori_loop(0, model // col_tile, step, 0)
            if 3 * j + 2 + n_slots < 3 * n_local:
                w_copy(3 * j + 2 + n_slots).start()
            continue
        for k in range(n_head):
            chunk = lax.rem(h + 1 + k, n_head)

            def step(i, carry):
                down(pl.ds(pl.multiple_of(chunk * width + i * col_tile, col_tile), col_tile))
                return carry

            lax.fori_loop(0, per, step, 0)
            cols = pl.ds(pl.multiple_of(chunk * width, LANES), width)
            obf[k] = acc[tp, :, :, cols].astype(BF16)
            c = send(obf.at[k], tin.at[k], to_s.at[k], to_r.at[k], on_tok)
            c.start()
            to_c.append(c)

    ho_c = []
    for k in range(n_head):
        chunk = lax.rem(h + 1 + k, n_head)
        cols = pl.ds(pl.multiple_of(chunk * width, LANES), width)
        to_c[k].wait_recv()
        if k < n_head - 1:
            hsend[k] = (acc[t, :, :, cols] + tin[k].astype(F32)).astype(BF16)
            c = send(hsend.at[k], hrecv.at[k], ho_s.at[k], ho_r.at[k], on_head(k + 1))
            c.start()
            ho_c.append(c)
    for c in ho_c:
        c.wait_recv()

    own = pl.ds(pl.multiple_of(h * width, LANES), width)

    def mixed(image):
        value = acc[t, image, :, own] + tin[n_head - 1, image].astype(F32)
        for k in range(n_head - 1):
            value = value + hrecv[k, image].astype(F32)
        return value

    zo_c = []
    for k in range(1, n_exp):
        zsend[k - 1] = mixed(lax.rem(e + k, n_exp)).astype(BF16)
        c = send(zsend.at[k - 1], zrecv.at[k - 1], zo_s.at[k], zo_r.at[k], on_exp(k))
        c.start()
        zo_c.append(c)

    @pl.when(jnp.logical_not(mine))
    def _():
        attn_c.wait()

    @pl.when(mine)
    def _():
        attn_in[...] = attn_buf[...]

    value = mixed(e) + (stream_ref[...] + attn_in[...])
    for k in range(1, n_exp):
        zo_c[k - 1].wait_recv()
        value = value + zrecv[k - 1].astype(F32)
    out_ref[...] = value
    for c in xz_c + qz_c + [c for _, _, c in xh_c] + qh_c + xt_c + to_c + ho_c + zo_c:
        c.wait_send()


def solution(mesh):
    n_tok, n_head, n_exp = mesh.shape["tok"], mesh.shape["head"], mesh.shape["exp"]

    def on_device(
        context, out_proj, stream, norm_gain, expert_ids, slot_ids, gate_probs, w_gate, w_up, w_down
    ):
        rows, width = stream.shape[1:]
        n_local, n_hid, model = w_gate.shape
        n_slots = min(3 * n_local, SLOT_BYTES // (n_hid * model * 2))
        tokens = n_tok * n_exp * rows
        hid_tile = 256 if n_hid % 256 == 0 else n_hid
        vmem = pl.BlockSpec(memory_space=pltpu.VMEM)
        hbm = pl.BlockSpec(memory_space=pl.ANY)
        dma = pltpu.SemaphoreType.DMA
        V = pltpu.VMEM
        scratch = [
            V(out_proj.shape, BF16),
            V((n_slots, n_hid, model), BF16),
            V((n_exp, rows, context.shape[2]), BF16),
            V((n_tok, n_exp, rows, LANES), F32),
            V((rows, width), BF16),
            V((rows, width), BF16),
            V((n_exp, rows, width), BF16),
            V((n_exp, rows, width), F32),
            V((n_head - 1, rows, width), BF16),
            V((rows, width), F32),
            V((rows, width), F32),
            V((n_tok, n_exp, n_exp, 8, LANES), F32),
            V((n_tok, n_exp, rows, model), BF16),
            V((n_hid // hid_tile, tokens, hid_tile), BF16),
            V((n_tok, n_exp, rows, model), F32),
            V((n_head, n_exp, rows, width), BF16),
            V((n_head, n_exp, rows, width), BF16),
            V((n_head - 1, n_exp, rows, width), BF16),
            V((n_head - 1, n_exp, rows, width), BF16),
            V((n_exp - 1, rows, width), BF16),
            V((n_exp - 1, rows, width), BF16),
            dma, dma((n_slots,)),
            dma((n_exp,)), dma((n_exp,)), dma((n_exp,)), dma((n_exp,)), dma, dma, dma, dma,
            dma((n_head,)), dma((n_head,)), dma, dma,
            dma((n_exp,)), dma((n_exp,)), dma((n_exp,)), dma((n_exp,)),
            dma((n_head, n_exp)), dma((n_head, n_exp)), dma((n_head,)), dma((n_head,)),
            dma((n_head,)), dma((n_head,)), dma((n_head,)), dma((n_head,)),
            dma((n_head,)), dma((n_head,)), dma((n_head,)), dma((n_head,)),
            dma((n_exp,)), dma((n_exp,)),
        ]
        out = pl.pallas_call(
            functools.partial(kernel, n_tok, n_head, n_exp, n_slots),
            out_shape=jax.ShapeDtypeStruct((rows, width), F32),
            in_specs=[vmem, hbm, vmem, vmem, vmem, vmem, vmem, hbm, hbm, hbm],
            out_specs=vmem,
            scratch_shapes=scratch,
            compiler_params=pltpu.CompilerParams(
                collective_id=0, has_side_effects=True, vmem_limit_bytes=67_043_328
            ),
        )(
            context[0], out_proj, stream[0], norm_gain[None], expert_ids[0], slot_ids[0],
            gate_probs[0], w_gate, w_up, w_down,
        )
        return out[None]

    in_specs = (
        P("exp", "tok", "head"),
        P("head", "exp"),
        P("exp", "tok", "head"),
        P(),
        P("exp", "tok", None),
        P("exp", "tok", None),
        P("exp", "tok", None),
        P(("tok", "exp"), "head", None),
        P(("tok", "exp"), "head", None),
        P(("tok", "exp"), "head", None),
    )
    return jax.shard_map(
        on_device, mesh=mesh, in_specs=in_specs, out_specs=P("exp", "tok", "head"), check_vma=False
    )
```

```python
import functools

import jax
import jax.numpy as jnp
from jax import lax
from jax.experimental import pallas as pl
from jax.experimental.pallas import tpu as pltpu
from jax.sharding import PartitionSpec as P

MESH = pl.DeviceIdType.MESH
LANES = 128
SLOT_BYTES = 50_400_000
F32 = jnp.float32
BF16 = jnp.bfloat16
eps_value = 1e-05


def kernel(
    n_tok, n_head, n_exp, n_slots,
    ctx_ref, proj_hbm, stream_ref, gain_ref, ids_ref, slots_ref, probs_ref,
    wg_hbm, wu_hbm, wd_hbm,
    out_ref,
    proj, wbuf, ctx_all, wall, stream_bf, stream_t, pbf, pown, prs,
    attn_buf, attn_in, ssq, x, hid, acc, obf, tin, hsend, hrecv, zsend, zrecv,
    proj_sem, w_sem, ctx_s, ctx_r, wz_s, wz_r, wt_s, wt_r, st_s, st_r,
    prs_s, prs_r, at_s, at_r, xz_s, xz_r, qz_s, qz_r, xh_s, xh_r, qh_s, qh_r,
    xt_s, xt_r, qt_s, qt_r, to_s, to_r, ho_s, ho_r, zo_s, zo_r,
):
    t, h, e = lax.axis_index("tok"), lax.axis_index("head"), lax.axis_index("exp")
    rows, width = stream_ref.shape
    n_local, n_hid, model = wg_hbm.shape
    tokens = n_tok * n_exp * rows
    tp = 1 - t
    turned = {"tok": t, "head": e, "exp": h}
    mine = h == e

    def send(src, dst, s_sem, r_sem, device):
        return pltpu.make_async_remote_copy(
            src_ref=src, dst_ref=dst, send_sem=s_sem, recv_sem=r_sem,
            device_id=device, device_id_type=MESH,
        )

    def on_exp(k):
        return {"exp": lax.rem(e + k, n_exp)}

    def on_head(k):
        return {"head": lax.rem(h + k, n_head)}

    on_tok = {"tok": tp}

    sources = [s.at[j] for j in range(n_local) for s in (wg_hbm, wu_hbm)]
    sources += [wd_hbm.at[j] for j in range(n_local)]

    def w_copy(q):
        return pltpu.make_async_copy(sources[q], wbuf.at[q % n_slots], w_sem.at[q % n_slots])

    proj_copy = pltpu.make_async_copy(proj_hbm, proj, proj_sem)
    proj_copy.start()

    barrier = pltpu.get_barrier_semaphore()
    for k in range(1, n_exp):
        pl.semaphore_signal(barrier, inc=1, device_id=on_exp(k), device_id_type=MESH)
    for k in range(1, n_head):
        pl.semaphore_signal(barrier, inc=1, device_id=on_head(k), device_id_type=MESH)
    pl.semaphore_signal(barrier, inc=1, device_id=on_tok, device_id_type=MESH)

    @pl.when(jnp.logical_not(mine))
    def _():
        pl.semaphore_signal(barrier, inc=1, device_id=turned, device_id_type=MESH)

    stream_bf[...] = stream_ref[...].astype(BF16)
    lane = lax.broadcasted_iota(jnp.int32, (rows, LANES), 1)
    n_experts = wall.shape[2]
    expert_row = lax.broadcasted_iota(jnp.int32, (n_experts, rows), 0)
    dense = jnp.zeros((n_experts, rows), F32)
    for k in range(ids_ref.shape[0]):
        hit = (ids_ref[k : k + 1, :] == expert_row) & (slots_ref[k : k + 1, :] >= 0)
        dense = dense + jnp.where(hit, probs_ref[k : k + 1, :], 0.0)
    wall[0, e] = jnp.zeros((n_experts, LANES), F32)
    wall[0, e, :, :rows] = dense
    ctx_all[e] = ctx_ref[...]

    @pl.when(mine)
    def _():
        pl.semaphore_wait(barrier, n_exp - 1 + n_head - 1 + 1)

    @pl.when(jnp.logical_not(mine))
    def _():
        pl.semaphore_wait(barrier, n_exp - 1 + n_head - 1 + 2)

    ctx_c = [
        send(ctx_ref, ctx_all.at[e], ctx_s.at[k], ctx_r.at[k], on_exp(k)) for k in range(1, n_exp)
    ]
    for c in ctx_c:
        c.start()
    stream_c = send(stream_bf, stream_t, st_s, st_r, turned)

    @pl.when(jnp.logical_not(mine))
    def _():
        stream_c.start()

    wz_c = [
        send(wall.at[0, e], wall.at[0, e], wz_s.at[k], wz_r.at[k], on_exp(k))
        for k in range(1, n_exp)
    ]
    for c in wz_c:
        c.start()
    proj_copy.wait()
    for c in ctx_c:
        c.wait()

    tile = min(width, 256)

    def project(i, carry):
        cols = pl.ds(pl.multiple_of(i * tile, tile), tile)
        part = jnp.dot(
            ctx_all[...].reshape(n_exp * rows, ctx_ref.shape[1]), proj[:, cols],
            preferred_element_type=F32,
        ).reshape(n_exp, rows, tile)
        pown[:, :, cols] = part
        pbf[:, :, cols] = part.astype(BF16)
        return carry

    lax.fori_loop(0, proj.shape[1] // tile, project, 0)
    prs_c = [
        send(
            pbf.at[lax.rem(h + k, n_head)], prs.at[k - 1], prs_s.at[k], prs_r.at[k], on_head(k)
        )
        for k in range(1, n_head)
    ]
    for c in prs_c:
        c.start()
    for q in range(n_slots):
        w_copy(q).start()
    for c in wz_c:
        c.wait()
    wt_c = send(wall.at[0], wall.at[1], wt_s, wt_r, on_tok)
    wt_c.start()

    @pl.when(jnp.logical_not(mine))
    def _():
        stream_c.wait()

    @pl.when(mine)
    def _():
        stream_t[...] = stream_bf[...]

    for c in prs_c:
        c.wait()
    attn = pown[h]
    for k in range(1, n_head):
        attn = attn + prs[k - 1].astype(F32)
    attn_buf[...] = attn
    attn_c = send(attn_buf, attn_in, at_s, at_r, turned)

    resid = attn + stream_t[...].astype(F32)
    gain = gain_ref[:, pl.ds(pl.multiple_of(e * width, LANES), width)]
    own_cols = pl.ds(pl.multiple_of(e * width, LANES), width)
    x[0, h, :, own_cols] = (resid * gain).astype(BF16)
    square = jnp.sum(resid * resid, axis=1, keepdims=True)
    row_id = lax.broadcasted_iota(jnp.int32, (rows, LANES), 0)
    flat = jnp.sum(jnp.where(row_id == lane, square, 0.0), axis=0, keepdims=True)
    ssq[0, h, e] = jnp.broadcast_to(flat, (8, LANES))

    def x_at(i, c):
        return x.at[0, i, :, pl.ds(pl.multiple_of(c * width, LANES), width)]

    xz_c = [
        send(x_at(h, e), x_at(h, e), xz_s.at[k], xz_r.at[k], on_exp(k)) for k in range(1, n_exp)
    ]
    qz_c = [
        send(ssq.at[0, h, e], ssq.at[0, h, e], qz_s.at[k], qz_r.at[k], on_exp(k))
        for k in range(1, n_exp)
    ]
    for a, b in zip(xz_c, qz_c):
        a.start()
        b.start()
    xh_c = []
    for j in range(n_exp):
        if j:
            xz_c[j - 1].wait_recv()
        piece = lax.rem(e - j + n_exp, n_exp)
        for k in range(1, n_head):
            c = send(x_at(h, piece), x_at(h, piece), xh_s.at[k, j], xh_r.at[k, j], on_head(k))
            c.start()
            xh_c.append((k, j, c))
    for c in qz_c:
        c.wait_recv()
    qh_c = [
        send(ssq.at[0, h], ssq.at[0, h], qh_s.at[k], qh_r.at[k], on_head(k))
        for k in range(1, n_head)
    ]
    for c in qh_c:
        c.start()

    @pl.when(jnp.logical_not(mine))
    def _():
        attn_c.start()

    xt_c = []
    for k in range(n_head):
        if k:
            for kk, j, c in xh_c:
                if kk == k:
                    c.wait_recv()
            qh_c[k - 1].wait_recv()
        image = lax.rem(h - k + n_head, n_head)
        a = send(x.at[0, image], x.at[1, image], xt_s.at[k], xt_r.at[k], on_tok)
        b = send(ssq.at[0, image], ssq.at[1, image], qt_s.at[k], qt_r.at[k], on_tok)
        a.start()
        b.start()
        xt_c += [a, b]
    for c in xt_c:
        c.wait_recv()
    wt_c.wait()

    token_row = lax.rem(lax.broadcasted_iota(jnp.int32, (tokens, LANES), 0), rows)
    token_lane = lax.broadcasted_iota(jnp.int32, (tokens, LANES), 1)

    def column(value):
        wide = jnp.broadcast_to(value, (n_tok, n_exp, rows, LANES)).reshape(tokens, LANES)
        return jnp.sum(jnp.where(token_row == token_lane, wide, 0.0), axis=1, keepdims=True)

    sums = column(jnp.sum(ssq[...], axis=2)[:, :, 0:1, :])
    scale = lax.rsqrt(sums / model + eps_value)
    expert_of = lax.broadcasted_iota(jnp.int32, wall.shape, 2)

    hid_tile = 256 if n_hid % 256 == 0 else n_hid
    col_tile = min(width, 512)
    per = width // col_tile

    n_tiles = n_hid // hid_tile
    for j in range(n_local):
        for m in range(2):
            w_copy(2 * j + m).wait()
        gs, us = (2 * j) % n_slots, (2 * j + 1) % n_slots
        number = (t * n_exp + e) * n_local + j
        picked = jnp.where(expert_of == number, wall[...], 0.0)
        gate_w = column(jnp.sum(picked, axis=2, keepdims=True))

        def up(i, carry):
            span = pl.ds(pl.multiple_of(i * hid_tile, hid_tile), hid_tile)
            dims = (((1,), (1,)), ((), ()))
            xv = x[...].reshape(tokens, model)
            g = lax.dot_general(xv, wbuf[gs, span, :], dims, preferred_element_type=F32) * scale
            u = lax.dot_general(xv, wbuf[us, span, :], dims, preferred_element_type=F32) * scale
            value = g / (1.0 + jnp.exp(-g)) * u * gate_w
            hid[j * n_tiles + i] = value.astype(BF16)
            return carry

        lax.fori_loop(0, n_tiles, up, 0)
        for m in range(2):
            if 2 * j + m + n_slots < 3 * n_local:
                w_copy(2 * j + m + n_slots).start()

    for j in range(n_local):
        w_copy(2 * n_local + j).wait()
    ho_c = []
    to_c = []

    def head_step(k):
        to_c[k].wait_recv()
        if k < n_head - 1:
            hsend[k] = (acc[k] + tin[k].astype(F32)).astype(BF16)
            c = send(hsend.at[k], hrecv.at[k], ho_s.at[k], ho_r.at[k], on_head(k + 1))
            c.start()
            ho_c.append(c)

    for k in range(n_head):
        chunk = lax.rem(h + 1 + k, n_head)

        def step(i, carry):
            part = pl.ds(pl.multiple_of(i * col_tile, col_tile), col_tile)
            cols = pl.ds(pl.multiple_of(chunk * width + i * col_tile, col_tile), col_tile)
            value = jnp.zeros((tokens, col_tile), F32)
            for j in range(n_local):
                for i in range(n_tiles):
                    value = value + jnp.dot(
                        hid[j * n_tiles + i],
                        wbuf[
                            (2 * n_local + j) % n_slots, i * hid_tile : (i + 1) * hid_tile, cols
                        ],
                        preferred_element_type=F32,
                    )
            value = value.reshape(n_tok, n_exp, rows, col_tile)
            acc[k, :, :, part] = value[0]
            obf[k, :, :, part] = value[1].astype(BF16)
            return carry

        lax.fori_loop(0, per, step, 0)
        c = send(obf.at[k], tin.at[k], to_s.at[k], to_r.at[k], on_tok)
        c.start()
        to_c.append(c)
        if k:
            head_step(k - 1)
    head_step(n_head - 1)

    for c in ho_c:
        c.wait_recv()


    def mixed(image):
        value = acc[n_head - 1, image] + tin[n_head - 1, image].astype(F32)
        for k in range(n_head - 1):
            value = value + hrecv[k, image].astype(F32)
        return value

    zo_c = []
    for k in range(1, n_exp):
        zsend[k - 1] = mixed(lax.rem(e + k, n_exp)).astype(BF16)
        c = send(zsend.at[k - 1], zrecv.at[k - 1], zo_s.at[k], zo_r.at[k], on_exp(k))
        c.start()
        zo_c.append(c)

    @pl.when(jnp.logical_not(mine))
    def _():
        attn_c.wait()

    @pl.when(mine)
    def _():
        attn_in[...] = attn_buf[...]

    value = mixed(e) + attn_in[...]
    for k in range(1, n_exp):
        zo_c[k - 1].wait_recv()
        value = value + zrecv[k - 1].astype(F32)
    out_ref[...] = value
    for c in xz_c + qz_c + [c for _, _, c in xh_c] + qh_c + xt_c + to_c + ho_c + zo_c:
        c.wait_send()


def solution(mesh):
    n_tok, n_head, n_exp = mesh.shape["tok"], mesh.shape["head"], mesh.shape["exp"]

    def on_device(
        context, out_proj, stream, norm_gain, expert_ids, slot_ids, gate_probs, w_gate, w_up, w_down
    ):
        rows, width = stream.shape[1:]
        n_local, n_hid, model = w_gate.shape
        n_slots = min(3 * n_local, SLOT_BYTES // (n_hid * model * 2))
        tokens = n_tok * n_exp * rows
        hid_tile = 256 if n_hid % 256 == 0 else n_hid
        vmem = pl.BlockSpec(memory_space=pltpu.VMEM)
        hbm = pl.BlockSpec(memory_space=pl.ANY)
        dma = pltpu.SemaphoreType.DMA
        V = pltpu.VMEM
        scratch = [
            V(out_proj.shape, BF16),
            V((n_slots, n_hid, model), BF16),
            V((n_exp, rows, context.shape[2]), BF16),
            V((n_tok, n_exp, n_tok * n_exp * n_local, LANES), F32),
            V((rows, width), BF16),
            V((rows, width), BF16),
            V((n_exp, rows, width), BF16),
            V((n_exp, rows, width), F32),
            V((n_head - 1, rows, width), BF16),
            V((rows, width), F32),
            V((rows, width), F32),
            V((n_tok, n_exp, n_exp, 8, LANES), F32),
            V((n_tok, n_exp, rows, model), BF16),
            V((n_local * (n_hid // hid_tile), tokens, hid_tile), BF16),
            V((n_head, n_exp, rows, width), F32),
            V((n_head, n_exp, rows, width), BF16),
            V((n_head, n_exp, rows, width), BF16),
            V((n_head - 1, n_exp, rows, width), BF16),
            V((n_head - 1, n_exp, rows, width), BF16),
            V((n_exp - 1, rows, width), BF16),
            V((n_exp - 1, rows, width), BF16),
            dma, dma((n_slots,)),
            dma((n_exp,)), dma((n_exp,)), dma((n_exp,)), dma((n_exp,)), dma, dma, dma, dma,
            dma((n_head,)), dma((n_head,)), dma, dma,
            dma((n_exp,)), dma((n_exp,)), dma((n_exp,)), dma((n_exp,)),
            dma((n_head, n_exp)), dma((n_head, n_exp)), dma((n_head,)), dma((n_head,)),
            dma((n_head,)), dma((n_head,)), dma((n_head,)), dma((n_head,)),
            dma((n_head,)), dma((n_head,)), dma((n_head,)), dma((n_head,)),
            dma((n_exp,)), dma((n_exp,)),
        ]
        out = pl.pallas_call(
            functools.partial(kernel, n_tok, n_head, n_exp, n_slots),
            out_shape=jax.ShapeDtypeStruct((rows, width), F32),
            in_specs=[vmem, hbm, vmem, vmem, vmem, vmem, vmem, hbm, hbm, hbm],
            out_specs=vmem,
            scratch_shapes=scratch,
            compiler_params=pltpu.CompilerParams(
                collective_id=0, has_side_effects=True, vmem_limit_bytes=67_043_328
            ),
        )(
            context[0], out_proj, stream[0], norm_gain[None], expert_ids[0].T, slot_ids[0].T,
            gate_probs[0].T, w_gate, w_up, w_down,
        )
        return stream + out[None]

    in_specs = (
        P("exp", "tok", "head"),
        P("head", "exp"),
        P("exp", "tok", "head"),
        P(),
        P("exp", "tok", None),
        P("exp", "tok", None),
        P("exp", "tok", None),
        P(("tok", "exp"), "head", None),
        P(("tok", "exp"), "head", None),
        P(("tok", "exp"), "head", None),
    )
    return jax.shard_map(
        on_device, mesh=mesh, in_specs=in_specs, out_specs=P("exp", "tok", "head"), check_vma=False
    )
```
